128 devices in a mesh: layer: 4 (over y_lo, core), shard: 32 (over z, y_hi, x).
Axes of the slice: x: 4, y: 4 (y_hi: 2, y_lo: 2; y = y_hi * 2 + y_lo), z: 4, core: 2. Of those that a mesh axis runs over, the one named last changes fastest.
Arguments:
- input_acts: bfloat16 [8, 16384, 5120], P('layer', 'shard'), may hold values from -6 to 6
- output_grads: bfloat16 [8, 16384, 1024], P('layer', 'shard'), may hold values from -6 to 6
- input_inverse: bfloat16 [8, 5120, 5120], P('layer', 'shard'), may hold values from -1 to 2, as said below
- output_inverse: bfloat16 [8, 1024, 1024], P('layer', 'shard'), may hold values from -1 to 2, as said below
- query_input: bfloat16 [8, 5120, 512], P(None, 'shard'), may hold values from -0.0048828125 to 0.0048828125
- query_output: bfloat16 [8, 1024, 512], P(None, 'shard'), may hold values from -0.1875 to 0.1875
- layer_order: int32 [8], replicated, may hold values from 0 to 7, each once
Outputs:
- scores: float32 [16384, 16], P('shard', 'layer')
The draws below stay inside these ranges and needn't reach their ends.
Inputs may be any that keep to these rules, and one draw needn't show every extreme that they name: `input_inverse`: symmetric in its last two dimensions, with a unit-sized diagonal. `output_inverse`: symmetric in its last two dimensions, with a unit-sized diagonal.
All inputs are finite; a program needn't handle non-finite values.
Results may differ from the reference program's by a relative error of at most 0.0045.
Values may be sent and summed in bfloat16 or wider, within the bound.
A program may use at most 128 MiB of HBM per device.

```python
import jax
import jax.numpy as jnp
from jax import lax

DIN = 5120
DOUT = 1024
QUERIES = 16
RANK = 32
LAYERS = 8
TOKENS = 16384


def symmetric_draw(key, width):
    raw = jax.random.truncated_normal(key, -4.0, 4.0, (LAYERS, width, width), jnp.float32)
    paired = (raw + jnp.swapaxes(raw, 1, 2)) * 0.7071
    result = jnp.eye(width, dtype=jnp.float32)[None] + 0.4 / jnp.sqrt(jnp.float32(width)) * paired
    return result.astype(jnp.bfloat16)


def draw_input_inverse(key, part):
    return symmetric_draw(jax.random.fold_in(key, 11), DIN)


def draw_output_inverse(key, part):
    return symmetric_draw(jax.random.fold_in(key, 13), DOUT)


def block_levels(stream_key, shape, cuts, least, top_value):
    gain = 1.0
    for dim, blocks in cuts:
        heights = jax.random.uniform(jax.random.fold_in(jax.random.fold_in(stream_key, 6), dim), (blocks,), jnp.float32, least / len(cuts), top_value / len(cuts))
        gain = gain * jnp.repeat(jnp.exp(heights), shape[dim] // blocks).reshape((-1,) + (1,) * (len(shape) - 1 - dim))
    return gain


def gaussian(own_key, dims, deviation, reach, split=(), kind=jnp.bfloat16):
    gain = block_levels(own_key, dims, split, -0.22, 0.18) if split else 1.0
    values = jax.random.normal(own_key, dims, jnp.float32) * deviation * gain
    return jnp.minimum(jnp.maximum(values, -reach), reach).astype(kind)


def setup_inputs(seed: int = 0) -> dict:
    key_of = jax.random.split(jax.random.key(seed), 8)
    return {
        "input_acts": gaussian(key_of[0], (LAYERS, TOKENS, DIN), 1.0, 6.0, ((0, 4), (1, 32))),
        "output_grads": gaussian(key_of[1], (LAYERS, TOKENS, DOUT), 1.0, 6.0, ((0, 4), (1, 32))),
        "input_inverse": draw_input_inverse(jax.random.fold_in(key_of[7], 71), 0),
        "output_inverse": draw_output_inverse(jax.random.fold_in(key_of[7], 71), 0),
        "query_input": gaussian(key_of[4], (LAYERS, DIN, QUERIES * RANK), (DIN * RANK * LAYERS) ** -0.5, 0.0048828125, ((1, 32),)),
        "query_output": gaussian(key_of[5], (LAYERS, DOUT, QUERIES * RANK), DOUT ** -0.5, 0.1875, ((1, 32),)),
        "layer_order": jax.random.permutation(key_of[6], LAYERS).astype(jnp.int32),
    }


def reference(input_acts, output_grads, input_inverse, output_inverse, query_input, query_output, layer_order):
    highest = lax.Precision.HIGHEST
    scores = jnp.zeros((TOKENS, QUERIES), jnp.float32)
    for position in range(LAYERS):
        model_layer = layer_order[position].astype(jnp.int32)
        vectors_in = lax.dynamic_index_in_dim(query_input, model_layer, 0, keepdims=False).astype(jnp.float32)
        vectors_out = lax.dynamic_index_in_dim(query_output, model_layer, 0, keepdims=False).astype(jnp.float32)
        folded_in = jnp.dot(input_inverse[position].astype(jnp.float32), vectors_in, precision=highest).astype(jnp.bfloat16)
        folded_out = jnp.dot(output_inverse[position].astype(jnp.float32), vectors_out, precision=highest).astype(jnp.bfloat16)
        left = jnp.dot(input_acts[position].astype(jnp.float32), folded_in.astype(jnp.float32), precision=highest)
        right = jnp.dot(output_grads[position].astype(jnp.float32), folded_out.astype(jnp.float32), precision=highest)
        scores = scores + (left * right).reshape(TOKENS, QUERIES, RANK).sum(axis=2)
    return scores
```

```python
import functools

import jax
import jax.numpy as jnp
from jax import lax
from jax.experimental import pallas as pl
from jax.experimental.pallas import tpu as pltpu
from jax.sharding import PartitionSpec as P

MESH = pl.DeviceIdType.MESH
BF16 = jnp.bfloat16
F32 = jnp.float32

DIN = 5120
DOUT = 1024
WIDTH = 512
HALF = 256
SLOTS = 2
TOK = 512
RI = 160
RO = 32

JOBS = 12


def dot(a, b):
    return jnp.dot(a, b, preferred_element_type=F32)


def kernel(
    order, q_hbm, qo_hbm, a_hbm, g_hbm, h_hbm, ho_hbm, out,
    q_all, qo_all, qg, qog, hb, hob, part_s, part_r, parto_s, parto_r, own, owno,
    pre, preo, acts, grads, left, right, score, score_r,
    ss, rs, ls,
):
    group = lax.axis_index("layer")
    shard = lax.axis_index("shard")
    ylo, core = lax.div(group, 2), lax.rem(group, 2)
    z, yhi, x = lax.div(shard, 8), lax.rem(lax.div(shard, 4), 2), lax.rem(shard, 4)
    other = 1 - yhi

    def device(zz, yy, xx):
        return (group, zz * 8 + yy * 4 + xx)

    def turn(i, by):
        return lax.rem(i + by + 4, 4)

    near = {
        ("x", 1): device(z, yhi, turn(x, 1)),
        ("x", -1): device(z, yhi, turn(x, -1)),
        ("z", 1): device(turn(z, 1), yhi, x),
        ("z", -1): device(turn(z, -1), yhi, x),
    }
    across = device(z, other, x)
    mates = [
        (ylo * 2 + 1 - core, shard),
        ((1 - ylo) * 2 + core, shard),
        ((1 - ylo) * 2 + 1 - core, shard),
    ]
    sent = []
    ids = {}

    def sem(name):
        return ids.setdefault(name, len(ids))

    def send(name, src, dst, to):
        k = sem(name)
        copy = pltpu.make_async_remote_copy(
            src_ref=src, dst_ref=dst, send_sem=ss.at[k], recv_sem=rs.at[k],
            device_id=to, device_id_type=MESH,
        )
        copy.start()
        sent.append(copy)

    def recv(name, ref):
        k = sem(name)
        pltpu.make_async_remote_copy(
            src_ref=ref, dst_ref=ref, send_sem=ss.at[k], recv_sem=rs.at[k],
            device_id=across, device_id_type=MESH,
        ).wait_recv()

    local = {}

    def fetch(name, src, dst):
        copy = pltpu.make_async_copy(src, dst, ls.at[len(local)])
        copy.start()
        local[name] = copy

    def ready(name):
        local[name].wait()

    class Gather:
        def __init__(self, name, first, at, half):
            self.name, self.at, self.half = name, at, half
            self.first, self.second = first, "z" if first == "x" else "x"
            self.i, self.j = (x, z) if first == "x" else (z, x)

        def place(self, i, j):
            return self.at(j, i) if self.first == "x" else self.at(i, j)

        def block(self, i, part):
            return self.half(self.place(i, self.j), part)

        def line(self, j, part):
            return self.place(pl.ds(2 * part, 2), j)

        def key(self, *k):
            return (self.name, *k)

        def first_send(self):
            for by, parts in ((1, (0, 1)), (-1, (1, 0))):
                for part in parts:
                    ref = self.block(self.i, part)
                    send(self.key("a", by, part), ref, ref, near[self.first, by])

        def first_pass(self):
            for by, part in ((1, 0), (-1, 1)):
                ref = self.block(turn(self.i, -by), part)
                recv(self.key("a", by, part), ref)
                send(self.key("b", by), ref, ref, near[self.first, by])

        def first_end(self):
            for by, part in ((1, 1), (-1, 0)):
                recv(self.key("a", by, part), self.block(turn(self.i, -by), part))
            for by, part in ((1, 0), (-1, 1)):
                recv(self.key("b", by), self.block(turn(self.i, 2), part))

        def second_send(self):
            for by, parts in ((1, (0, 1)), (-1, (1, 0))):
                for part in parts:
                    ref = self.line(self.j, part)
                    send(self.key("c", by, part), ref, ref, near[self.second, by])

        def second_pass(self):
            for by, part in ((1, 0), (-1, 1)):
                ref = self.line(turn(self.j, -by), part)
                recv(self.key("c", by, part), ref)
                send(self.key("d", by), ref, ref, near[self.second, by])

        def second_end(self):
            for by, part in ((1, 1), (-1, 0)):
                recv(self.key("c", by, part), self.line(turn(self.j, -by), part))
            for by, part in ((1, 0), (-1, 1)):
                recv(self.key("d", by), self.line(turn(self.j, 2), part))

    rows = lambda ref, part: ref.at[..., pl.ds(RI // 2 * part, RI // 2), :]
    slots = lambda ref, part: ref.at[..., pl.ds(part, 1), :, :]
    axes = ("x", "z")

    def pair(make):
        return [make(h) for h in range(2)]

    def q_job(p):
        return pair(lambda h: Gather(("q", p, h), axes[h], lambda zz, xx: qg.at[p, h, zz, xx], rows))

    def p_job(p):
        return pair(lambda h: Gather(("p", p, h), axes[h], lambda zz, xx: pre.at[p, h, zz, :, xx], rows))

    qo_job = pair(lambda h: Gather(("qo", h), axes[h], lambda zz, xx: qog.at[h, zz, xx], slots))
    po_job = pair(lambda h: Gather(("po", h), axes[h], lambda zz, xx: preo.at[h, zz, :, xx], slots))
    q_jobs, p_jobs = [q_job(0), q_job(1)], [p_job(0), p_job(1)]

    def do(step, job):
        for gather in job:
            getattr(gather, step)()

    def columns(ref, p, zz, yy, width):
        return ref.at[p, :, pl.ds(pl.multiple_of((zz * 2 + yy) * width, width), width)]

    fetch("q", q_hbm, q_all)
    fetch("qo", qo_hbm, qo_all)
    barrier = pltpu.get_barrier_semaphore()
    peers = list(near.values()) + [across] + mates
    for peer in peers:
        pl.semaphore_signal(barrier, inc=1, device_id=peer, device_id_type=MESH)

    for p in range(SLOTS):
        for zz in range(4):
            fetch(("h", p, zz), columns(h_hbm, p, zz, yhi, 4 * RI), hb.at[p, zz, pl.ds(0, RI)])
            fetch(("ho", p, zz), columns(ho_hbm, p, zz, yhi, 4 * RO), hob.at[p, zz, pl.ds(0, RO)])

    def share_h(p, zz):
        send(("h", p, zz), columns(h_hbm, p, zz, other, 4 * RI), hb.at[p, zz, pl.ds(RI, RI)], across)

    def got_h(p):
        for zz in range(4):
            ready(("h", p, zz))
            recv(("h", p, zz), hb.at[p, zz, pl.ds(RI, RI)])

    ready("q")
    ready("qo")
    for p in range(SLOTS):
        m = order[group * SLOTS + p]
        for h in range(2):
            qg[p, h, z, x] = q_all[m, :, pl.ds(h * HALF, HALF)]
            qog[h, z, x, p] = qo_all[m, :, pl.ds(h * HALF, HALF)]

    pl.semaphore_wait(barrier, len(peers))
    do("first_send", q_jobs[0])
    for zz in range(4):
        share_h(0, zz)
    do("first_send", q_jobs[1])
    for p in range(SLOTS):
        for zz in range(4):
            fetch(("a", p, zz), a_hbm.at[p, :, pl.ds(zz * 8 * RI, 8 * RI)], acts.at[p, zz])
    fetch("g", g_hbm, grads)

    def share_part(p):
        got_h(p)
        for h in range(2):
            def add(zz, acc):
                return acc + dot(hb[p, zz], qg[p, h, zz].reshape(4 * RI, HALF))
            acc = lax.fori_loop(0, 4, add, jnp.zeros((2 * RI, HALF), F32))
            own[p, h] = acc[:RI]
            part_s[p, h] = acc[RI:].astype(BF16)
            send(("part", p, h), part_s.at[p, h], part_r.at[p, h], across)

    def share_pre(p):
        for h in range(2):
            recv(("part", p, h), part_r.at[p, h])
            pre[p, h, z, yhi, x] = (own[p, h] + part_r[p, h].astype(F32)).astype(BF16)
            ref = pre.at[p, h, z, yhi, x]
            send(("y", p, h), ref, ref, across)

    def got_pre(p):
        for h in range(2):
            recv(("y", p, h), pre.at[p, h, z, other, x])

    def share_h_out():
        for p in range(SLOTS):
            for zz in range(4):
                send(("ho", p, zz), columns(ho_hbm, p, zz, other, 4 * RO), hob.at[p, zz, pl.ds(RO, RO)], across)

    def share_part_out():
        for p in range(SLOTS):
            for zz in range(4):
                ready(("ho", p, zz))
                recv(("ho", p, zz), hob.at[p, zz, pl.ds(RO, RO)])
        for h in range(2):
            for p in range(SLOTS):
                acc = jnp.zeros((2 * RO, HALF), F32)
                for zz in range(4):
                    acc = acc + dot(hob[p, zz], qog[h, zz, :, p].reshape(4 * RO, HALF))
                owno[h, p] = acc[:RO]
                parto_s[h, p] = acc[RO:].astype(BF16)
            send(("parto", h), parto_s.at[h], parto_r.at[h], across)

    def share_pre_out():
        for h in range(2):
            recv(("parto", h), parto_r.at[h])
            preo[h, z, yhi, x] = (owno[h] + parto_r[h].astype(F32)).astype(BF16)
            ref = preo.at[h, z, yhi, x]
            send(("yo", h), ref, ref, across)

    def got_pre_out():
        for h in range(2):
            recv(("yo", h), preo.at[h, z, other, x])

    def make_left(p):
        for zz in range(4):
            ready(("a", p, zz))
        for h in range(2):
            left[p, h] = dot(acts[p, 0], pre[p, h, 0].reshape(8 * RI, HALF))

            def add(zz, carry):
                left[p, h] += dot(acts[p, zz], pre[p, h, zz].reshape(8 * RI, HALF))
                return carry
            lax.fori_loop(1, 4, add, 0)

    def make_right():
        ready("g")
        for p in range(SLOTS):
            for h in range(2):
                right[p, h] = dot(grads[p], preo[h, :, :, :, p].reshape(DOUT, HALF))

    do("first_pass", q_jobs[0])
    do("first_end", q_jobs[0])
    do("second_send", q_jobs[0])
    share_h_out()
    do("first_pass", q_jobs[1])
    do("first_send", qo_job)
    do("second_pass", q_jobs[0])
    do("first_end", q_jobs[1])
    do("second_send", q_jobs[1])
    do("first_pass", qo_job)
    do("second_end", q_jobs[0])
    share_part(0)
    for zz in range(4):
        share_h(1, zz)
    do("second_pass", q_jobs[1])
    do("first_end", qo_job)
    do("second_send", qo_job)
    share_pre(0)
    do("second_pass", qo_job)
    do("second_end", q_jobs[1])
    got_pre(0)
    do("first_send", p_jobs[0])
    do("second_end", qo_job)
    share_part_out()
    do("first_pass", p_jobs[0])
    share_pre_out()
    do("first_end", p_jobs[0])
    do("second_send", p_jobs[0])
    got_pre_out()
    do("first_send", po_job)
    do("first_pass", po_job)
    share_part(1)
    do("second_pass", p_jobs[0])
    do("first_end", po_job)
    do("second_send", po_job)
    share_pre(1)
    got_pre(1)
    do("first_send", p_jobs[1])
    do("second_pass", po_job)
    do("second_end", p_jobs[0])
    do("first_pass", p_jobs[1])
    do("first_end", p_jobs[1])
    do("second_send", p_jobs[1])
    do("second_end", po_job)
    make_left(0)
    do("second_pass", p_jobs[1])
    make_right()
    do("second_end", p_jobs[1])
    make_left(1)

    r = lax.broadcasted_iota(jnp.int32, (16, HALF), 0)
    c = lax.broadcasted_iota(jnp.int32, (16, HALF), 1)
    first = c // 32 * 2 - c // 128 * 8
    pick = (r // 8 == c // 128) & ((r - r // 8 * 8) * 2 == first)
    pick = jnp.where(pick, 1.0, 0.0).astype(F32)
    for h in range(2):
        product = left[0, h] * right[0, h] + left[1, h] * right[1, h]
        sums = lax.dot_general(
            pick, product, (((1,), (1,)), ((), ())),
            precision=lax.Precision.HIGHEST, preferred_element_type=F32,
        )
        score[pl.ds(2 * h, 2)] = sums.reshape(2, 8, TOK)
    for k, mate in enumerate(mates):
        send(("s", k), score.at[mate[0]], score_r.at[k], mate)
    total = score[group]
    for k in range(3):
        recv(("s", k), score_r.at[k])
        total = total + score_r[k]
    out[...] = total
    for copy in sent:
        copy.wait_send()


def shards(input_acts, output_grads, input_inverse, output_inverse, query_input, query_output, layer_order):
    any_space = pl.BlockSpec(memory_space=pl.ANY)
    result = pl.pallas_call(
        kernel,
        out_shape=jax.ShapeDtypeStruct((8, TOK), F32),
        in_specs=[pl.BlockSpec(memory_space=pltpu.SMEM)] + [any_space] * 6,
        out_specs=pl.BlockSpec(memory_space=pltpu.VMEM),
        scratch_shapes=[
            pltpu.VMEM((8, RI, WIDTH), BF16),
            pltpu.VMEM((8, RO, WIDTH), BF16),
            pltpu.VMEM((SLOTS, 2, 4, 4, RI, HALF), BF16),
            pltpu.VMEM((2, 4, 4, SLOTS, RO, HALF), BF16),
            pltpu.VMEM((SLOTS, 4, 2 * RI, 4 * RI), BF16),
            pltpu.VMEM((SLOTS, 4, 2 * RO, 4 * RO), BF16),
            pltpu.VMEM((SLOTS, 2, RI, HALF), BF16),
            pltpu.VMEM((SLOTS, 2, RI, HALF), BF16),
            pltpu.VMEM((2, SLOTS, RO, HALF), BF16),
            pltpu.VMEM((2, SLOTS, RO, HALF), BF16),
            pltpu.VMEM((SLOTS, 2, RI, HALF), F32),
            pltpu.VMEM((2, SLOTS, RO, HALF), F32),
            pltpu.VMEM((SLOTS, 2, 4, 2, 4, RI, HALF), BF16),
            pltpu.VMEM((2, 4, 2, 4, SLOTS, RO, HALF), BF16),
            pltpu.VMEM((SLOTS, 4, TOK, 8 * RI), BF16),
            pltpu.VMEM((SLOTS, TOK, DOUT), BF16),
            pltpu.VMEM((SLOTS, 2, TOK, HALF), F32),
            pltpu.VMEM((SLOTS, 2, TOK, HALF), F32),
            pltpu.VMEM((4, 8, TOK), F32),
            pltpu.VMEM((3, 8, TOK), F32),
            pltpu.SemaphoreType.DMA((192,)),
            pltpu.SemaphoreType.DMA((192,)),
            pltpu.SemaphoreType.DMA((32,)),
        ],
        compiler_params=pltpu.CompilerParams(
            collective_id=0, has_side_effects=True, vmem_limit_bytes=56 * 2**20
        ),
    )(layer_order, query_input, query_output, input_acts, output_grads, input_inverse, output_inverse)
    return result[:4].T


def solution(mesh):
    in_specs = (
        P("layer", "shard", None),
        P("layer", "shard", None),
        P("layer", "shard", None),
        P("layer", "shard", None),
        P(None, "shard", None),
        P(None, "shard", None),
        P(),
    )
    return jax.shard_map(shards, mesh=mesh, in_specs=in_specs, out_specs=P("shard", "layer"), check_vma=False)
```

```python
import functools

import jax
import jax.numpy as jnp
from jax import lax
from jax.experimental import pallas as pl
from jax.experimental.pallas import tpu as pltpu
from jax.sharding import PartitionSpec as P

MESH = pl.DeviceIdType.MESH
BF16 = jnp.bfloat16
F32 = jnp.float32

DIN = 5120
DOUT = 1024
WIDTH = 512
HALF = 256
SLOTS = 2
TOK = 512
RI = 160
RO = 32

SENDS, RECEIVES, LOADS = 34, 96, 8


def dot(a, b):
    return jnp.dot(a, b, preferred_element_type=F32)


def kernel(
    order, q_hbm, qo_hbm, a_hbm, g_hbm, h_hbm, ho_hbm, out,
    q_all, qo_all, qg, qog, hb, hob, part_s, part_r, parto_s, parto_r, own, owno,
    pre, preo, acts, grads, left, right, score, score_r,
    ss, rs, ls,
):
    group = lax.axis_index("layer")
    shard = lax.axis_index("shard")
    ylo, core = lax.div(group, 2), lax.rem(group, 2)
    z, yhi, x = lax.div(shard, 8), lax.rem(lax.div(shard, 4), 2), lax.rem(shard, 4)
    other = 1 - yhi

    def device(zz, yy, xx):
        return (group, zz * 8 + yy * 4 + xx)

    def turn(i, by):
        return lax.rem(i + by + 4, 4)

    near = {
        ("x", 1): device(z, yhi, turn(x, 1)),
        ("x", -1): device(z, yhi, turn(x, -1)),
        ("z", 1): device(turn(z, 1), yhi, x),
        ("z", -1): device(turn(z, -1), yhi, x),
    }
    across = device(z, other, x)
    mates = [
        (ylo * 2 + 1 - core, shard),
        ((1 - ylo) * 2 + core, shard),
        ((1 - ylo) * 2 + 1 - core, shard),
    ]
    sends, receives, loads = {}, {}, {}

    def number(table, name):
        return table.setdefault(name, len(table))

    def send(name, into, src, dst, to):
        pltpu.make_async_remote_copy(
            src_ref=src, dst_ref=dst,
            send_sem=ss.at[number(sends, name)], recv_sem=rs.at[number(receives, into)],
            device_id=to, device_id_type=MESH,
        ).start()

    def wait(name, ref, arrival=True):
        copy = pltpu.make_async_remote_copy(
            src_ref=ref, dst_ref=ref,
            send_sem=ss.at[0 if arrival else number(sends, name)],
            recv_sem=rs.at[number(receives, name) if arrival else 0],
            device_id=across, device_id_type=MESH,
        )
        copy.wait_recv() if arrival else copy.wait_send()

    def left_here(name, ref):
        wait(name, ref, arrival=False)

    def fetch(name, src, dst):
        pltpu.make_async_copy(src, dst, ls.at[number(loads, name)]).start()

    def ready(name, ref):
        pltpu.make_async_copy(ref, ref, ls.at[number(loads, name)]).wait()

    class Gather:
        def __init__(self, name, first, at, half):
            self.name, self.at, self.half = name, at, half
            self.first, self.second = first, "z" if first == "x" else "x"
            self.i, self.j = (x, z) if first == "x" else (z, x)

        def place(self, i, j):
            return self.at(j, i) if self.first == "x" else self.at(i, j)

        def block(self, i, part):
            return self.half(self.place(i, self.j), part)

        def line(self, j, part):
            return self.place(pl.ds(2 * part, 2), j)

        def key(self, k):
            return (self.name, k)

        def first_send(self):
            for by, parts in ((1, (0, 1)), (-1, (1, 0))):
                for k, part in enumerate(parts):
                    ref = self.block(self.i, part)
                    send(self.key("f"), self.key("f" if k else by), ref, ref, near[self.first, by])

        def first_pass(self):
            for by, part in ((1, 0), (-1, 1)):
                ref = self.block(turn(self.i, -by), part)
                wait(self.key(by), ref)
                send(self.key("f"), self.key("f"), ref, ref, near[self.first, by])

        def first_end(self):
            wait(self.key("f"), self.place(pl.ds(0, 2), self.j))

        def second_send(self):
            for by, parts in ((1, (0, 1)), (-1, (1, 0))):
                for k, part in enumerate(parts):
                    ref = self.line(self.j, part)
                    send(self.key("s"), self.key("near" if k else 2 * by), ref, ref, near[self.second, by])

        def second_pass(self):
            for by, part in ((1, 0), (-1, 1)):
                ref = self.line(turn(self.j, -by), part)
                wait(self.key(2 * by), ref)
                send(self.key("s"), self.key("far"), ref, ref, near[self.second, by])

        def second_near(self):
            wait(self.key("near"), self.place(pl.ds(0, 4), self.j))

        def second_far(self):
            wait(self.key("far"), self.place(pl.ds(0, 4), self.j))

        def second_end(self):
            self.second_near()
            self.second_far()

        def finish(self):
            left_here(self.key("f"), self.place(pl.ds(0, 3), self.j))
            left_here(self.key("s"), self.place(pl.ds(0, 4), pl.ds(0, 3)))

    rows = lambda ref, part: ref.at[..., pl.ds(RI // 2 * part, RI // 2), :]
    slots = lambda ref, part: ref.at[..., pl.ds(part, 1), :, :]
    axes = ("x", "z")

    def pair(make):
        return [make(h) for h in range(2)]

    def q_job(p):
        return pair(lambda h: Gather(("q", p, h), axes[h], lambda zz, xx: qg.at[p, h, zz, xx], rows))

    def p_job(p):
        return pair(lambda h: Gather(("p", p, h), axes[h], lambda zz, xx: pre.at[p, h, zz, :, xx], rows))

    qo_job = pair(lambda h: Gather(("qo", h), axes[h], lambda zz, xx: qog.at[h, zz, xx], slots))
    po_job = pair(lambda h: Gather(("po", h), axes[h], lambda zz, xx: preo.at[h, zz, yhi, xx], slots))
    q_jobs, p_jobs = [q_job(0), q_job(1)], [p_job(0), p_job(1)]

    def do(step, job):
        for gather in job:
            getattr(gather, step)()

    def columns(ref, p, zz, yy, width):
        return ref.at[p, :, pl.ds(pl.multiple_of((zz * 2 + yy) * width, width), width)]

    fetch("qo", qo_hbm, qo_all)
    fetch("q", q_hbm, q_all)
    barrier = pltpu.get_barrier_semaphore()
    peers = list(near.values()) + [across] + mates
    for peer in peers:
        pl.semaphore_signal(barrier, inc=1, device_id=peer, device_id_type=MESH)
    h_own = [hb.at[p, :, pl.ds(0, RI)] for p in range(SLOTS)]
    h_other = [hb.at[p, :, pl.ds(RI, RI)] for p in range(SLOTS)]
    ho_own, ho_other = hob.at[:, :, pl.ds(0, RO)], hob.at[:, :, pl.ds(RO, RO)]
    for p in range(SLOTS):
        for zz in range(4):
            fetch("ho", columns(ho_hbm, p, zz, yhi, 4 * RO), ho_own.at[p, zz])
    for p in range(SLOTS):
        for zz in range(4):
            fetch(("h", p), columns(h_hbm, p, zz, yhi, 4 * RI), h_own[p].at[zz])

    def share_h(p):
        for zz in range(4):
            send(("h", p), ("h", p), columns(h_hbm, p, zz, other, 4 * RI), h_other[p].at[zz], across)

    def share_h_out():
        for p in range(SLOTS):
            for zz in range(4):
                send("ho", "ho", columns(ho_hbm, p, zz, other, 4 * RO), ho_other.at[p, zz], across)

    def share_part(p):
        ready(("h", p), h_own[p])
        wait(("h", p), h_other[p])
        for h in range(2):
            def add(zz, acc):
                return acc + dot(hb[p, zz], qg[p, h, zz].reshape(4 * RI, HALF))
            acc = lax.fori_loop(0, 4, add, jnp.zeros((2 * RI, HALF), F32))
            own[p, h] = acc[:RI]
            part_s[p, h] = acc[RI:].astype(BF16)
            send(("part", p), ("part", p, h), part_s.at[p, h], part_r.at[p, h], across)

    def share_pre(p):
        for h in range(2):
            wait(("part", p, h), part_r.at[p, h])
            pre[p, h, z, yhi, x] = (own[p, h] + part_r[p, h].astype(F32)).astype(BF16)
            ref = pre.at[p, h, z, yhi, x]
            send(("y", p), ("y", p), ref, ref, across)

    def got_pre(p):
        wait(("y", p), pre.at[p, :, z, other, x])

    def share_part_out():
        ready("ho", ho_own)
        wait("ho", ho_other)
        for h in range(2):
            for p in range(SLOTS):
                acc = jnp.zeros((2 * RO, HALF), F32)
                for zz in range(4):
                    acc = acc + dot(hob[p, zz], qog[h, zz, :, p].reshape(4 * RO, HALF))
                owno[h, p] = acc[:RO]
                parto_s[h, p] = acc[RO:].astype(BF16)
        send("parto", "parto", parto_s, parto_r, across)

    def make_pre_out():
        wait("parto", parto_r)
        for h in range(2):
            preo[h, z, yhi, x] = (owno[h] + parto_r[h].astype(F32)).astype(BF16)

    def share_pre_out():
        for h in range(2):
            ref = preo.at[h, :, yhi]
            send("yo", "yo", ref, ref, across)

    def add_left(p, h, zz):
        left[p, h] += dot(acts[p, zz], pre[p, h, zz].reshape(8 * RI, HALF))

    def start_left(p, h):
        left[p, h] = dot(acts[p, z], pre[p, h, z].reshape(8 * RI, HALF))

    def near_left(p, h):
        def add(k, carry):
            add_left(p, h, turn(z, 2 * k - 1))
            return carry
        lax.fori_loop(0, 2, add, 0)

    def far_left(p, h):
        add_left(p, h, turn(z, 2))

    def make_left(p, h):
        start_left(p, h)
        near_left(p, h)
        far_left(p, h)

    def got_acts(p):
        ready(("a", p), acts.at[p])

    def make_right():
        ready("g", grads)
        wait("yo", preo.at[:, :, other])
        for p in range(SLOTS):
            for h in range(2):
                right[p, h] = dot(grads[p], preo[h, :, :, :, p].reshape(DOUT, HALF))

    def place_q(p):
        m = order[group * SLOTS + p]
        for h in range(2):
            qg[p, h, z, x] = q_all[m, :, pl.ds(h * HALF, HALF)]

    def place_q_out():
        for p in range(SLOTS):
            m = order[group * SLOTS + p]
            for h in range(2):
                qog[h, z, x, p] = qo_all[m, :, pl.ds(h * HALF, HALF)]

    def load_rest():
        for p in range(SLOTS):
            for zz in range(4):
                fetch(("a", p), a_hbm.at[p, :, pl.ds(zz * 8 * RI, 8 * RI)], acts.at[p, zz])
        fetch("g", g_hbm, grads)

    schedule = [
        (pl.semaphore_wait, barrier, len(peers)),
        (share_h_out,),
        (share_h, 0),
        (ready, "qo", qo_all),
        (place_q_out,),
        (do, "first_send", qo_job),
        (ready, "q", q_all),
        (place_q, 0),
        (do, "first_send", q_jobs[0]),
        (place_q, 1),
        (do, "first_pass", qo_job),
        (do, "first_send", q_jobs[1]),
        (load_rest,),
        (do, "first_end", qo_job),
        (do, "second_send", qo_job),
        (do, "first_pass", q_jobs[0]),
        (do, "second_pass", qo_job),
        (do, "first_end", q_jobs[0]),
        (do, "second_send", q_jobs[0]),
        (do, "first_pass", q_jobs[1]),
        (do, "second_end", qo_job),
        (share_part_out,),
        (do, "first_end", q_jobs[1]),
        (do, "second_pass", q_jobs[0]),
        (do, "second_send", q_jobs[1]),
        (make_pre_out,),
        (do, "first_send", po_job),
        (do, "second_end", q_jobs[0]),
        (share_part, 0),
        (do, "first_pass", po_job),
        (do, "second_pass", q_jobs[1]),
        (do, "first_end", po_job),
        (do, "second_send", po_job),
        (share_pre, 0),
        (share_h, 1),
        (do, "second_pass", po_job),
        (got_pre, 0),
        (do, "first_send", p_jobs[0]),
        (do, "second_end", q_jobs[1]),
        (do, "second_end", po_job),
        (do, "first_pass", p_jobs[0]),
        (do, "first_end", p_jobs[0]),
        (do, "second_send", p_jobs[0]),
        (got_acts, 0),
        (got_acts, 1),
        (do, "second_pass", p_jobs[0]),
        (share_part, 1),
        (share_pre, 1),
        (share_pre_out,),
        (got_pre, 1),
        (do, "first_send", p_jobs[1]),
        (do, "second_end", p_jobs[0]),
        (do, "first_pass", p_jobs[1]),
        (do, "first_end", p_jobs[1]),
        (do, "second_send", p_jobs[1]),
        (make_left, 0, 0),
        (make_left, 0, 1),
        (do, "second_pass", p_jobs[1]),
        (start_left, 1, 0),
        (do, "second_near", p_jobs[1]),
        (near_left, 1, 0),
        (make_right,),
        (do, "second_far", p_jobs[1]),
        (far_left, 1, 0),
        (make_left, 1, 1),
    ]
    for step, *given in schedule:
        step(*given)

    r = lax.broadcasted_iota(jnp.int32, (16, HALF), 0)
    c = lax.broadcasted_iota(jnp.int32, (16, HALF), 1)
    first = c // 32 * 2 - c // 128 * 8
    pick = (r // 8 == c // 128) & ((r - r // 8 * 8) * 2 == first)
    pick = jnp.where(pick, 1.0, 0.0).astype(F32)
    for h in range(2):
        product = left[0, h] * right[0, h] + left[1, h] * right[1, h]
        sums = lax.dot_general(
            pick, product, (((1,), (1,)), ((), ())),
            precision=lax.Precision.HIGHEST, preferred_element_type=F32,
        )
        score[pl.ds(2 * h, 2)] = sums.reshape(2, 8, TOK)
    for k, mate in enumerate(mates):
        send("score", "score", score.at[mate[0]], score_r.at[k], mate)
    wait("score", score_r)
    out[...] = (score[group] + score_r[0]) + (score_r[1] + score_r[2])

    for job in [qo_job, po_job] + q_jobs + p_jobs:
        do("finish", job)
    for p in range(SLOTS):
        left_here(("h", p), h_other[p])
        left_here(("part", p), part_s.at[p])
        left_here(("y", p), pre.at[p, :, z, yhi, x])
    left_here("ho", ho_other)
    left_here("parto", parto_s)
    left_here("yo", preo.at[:, :, yhi])
    left_here("score", score_r)
    assert (len(sends), len(receives), len(loads)) == (SENDS, RECEIVES, LOADS)


def shards(input_acts, output_grads, input_inverse, output_inverse, query_input, query_output, layer_order):
    any_space = pl.BlockSpec(memory_space=pl.ANY)
    result = pl.pallas_call(
        kernel,
        out_shape=jax.ShapeDtypeStruct((8, TOK), F32),
        in_specs=[pl.BlockSpec(memory_space=pltpu.SMEM)] + [any_space] * 6,
        out_specs=pl.BlockSpec(memory_space=pltpu.VMEM),
        scratch_shapes=[
            pltpu.VMEM((8, RI, WIDTH), BF16),
            pltpu.VMEM((8, RO, WIDTH), BF16),
            pltpu.VMEM((SLOTS, 2, 4, 4, RI, HALF), BF16),
            pltpu.VMEM((2, 4, 4, SLOTS, RO, HALF), BF16),
            pltpu.VMEM((SLOTS, 4, 2 * RI, 4 * RI), BF16),
            pltpu.VMEM((SLOTS, 4, 2 * RO, 4 * RO), BF16),
            pltpu.VMEM((SLOTS, 2, RI, HALF), BF16),
            pltpu.VMEM((SLOTS, 2, RI, HALF), BF16),
            pltpu.VMEM((2, SLOTS, RO, HALF), BF16),
            pltpu.VMEM((2, SLOTS, RO, HALF), BF16),
            pltpu.VMEM((SLOTS, 2, RI, HALF), F32),
            pltpu.VMEM((2, SLOTS, RO, HALF), F32),
            pltpu.VMEM((SLOTS, 2, 4, 2, 4, RI, HALF), BF16),
            pltpu.VMEM((2, 4, 2, 4, SLOTS, RO, HALF), BF16),
            pltpu.VMEM((SLOTS, 4, TOK, 8 * RI), BF16),
            pltpu.VMEM((SLOTS, TOK, DOUT), BF16),
            pltpu.VMEM((SLOTS, 2, TOK, HALF), F32),
            pltpu.VMEM((SLOTS, 2, TOK, HALF), F32),
            pltpu.VMEM((4, 8, TOK), F32),
            pltpu.VMEM((3, 8, TOK), F32),
            pltpu.SemaphoreType.DMA((SENDS,)),
            pltpu.SemaphoreType.DMA((RECEIVES,)),
            pltpu.SemaphoreType.DMA((LOADS,)),
        ],
        compiler_params=pltpu.CompilerParams(
            collective_id=0, has_side_effects=True, vmem_limit_bytes=56 * 2**20
        ),
    )(layer_order, query_input, query_output, input_acts, output_grads, input_inverse, output_inverse)
    return result[:4].T


def solution(mesh):
    in_specs = (
        P("layer", "shard", None),
        P("layer", "shard", None),
        P("layer", "shard", None),
        P("layer", "shard", None),
        P(None, "shard", None),
        P(None, "shard", None),
        P(),
    )
    return jax.shard_map(shards, mesh=mesh, in_specs=in_specs, out_specs=P("shard", "layer"), check_vma=False)
```

```python
import functools

import jax
import jax.numpy as jnp
from jax import lax
from jax.experimental import pallas as pl
from jax.experimental.pallas import tpu as pltpu
from jax.sharding import PartitionSpec as P

MESH = pl.DeviceIdType.MESH
BF16 = jnp.bfloat16
F32 = jnp.float32

DIN = 5120
DOUT = 1024
WIDTH = 512
HALF = 256
SLOTS = 2
TOK = 512
RI = 160
RO = 32

SENDS, RECEIVES, LOADS = 42, 100, 8


def dot(a, b):
    return jnp.dot(a, b, preferred_element_type=F32)


def kernel(
    order, q_hbm, qo_hbm, a_hbm, g_hbm, h_hbm, ho_hbm, out,
    q_all, qo_all, qg, qog, hb, hob, part_s, part_r, parto_s, parto_r, own, owno,
    pre, preo, acts, grads, left, right, score, score_r,
    ss, rs, ls,
):
    group = lax.axis_index("layer")
    shard = lax.axis_index("shard")
    ylo, core = lax.div(group, 2), lax.rem(group, 2)
    z, yhi, x = lax.div(shard, 8), lax.rem(lax.div(shard, 4), 2), lax.rem(shard, 4)
    other = 1 - yhi

    def device(zz, yy, xx):
        return (group, zz * 8 + yy * 4 + xx)

    def turn(i, by):
        return lax.rem(i + by + 4, 4)

    near = {
        ("x", 1): device(z, yhi, turn(x, 1)),
        ("x", -1): device(z, yhi, turn(x, -1)),
        ("z", 1): device(turn(z, 1), yhi, x),
        ("z", -1): device(turn(z, -1), yhi, x),
    }
    across = device(z, other, x)
    mates = [
        (ylo * 2 + 1 - core, shard),
        ((1 - ylo) * 2 + core, shard),
        ((1 - ylo) * 2 + 1 - core, shard),
    ]
    sends, receives, loads = {}, {}, {}

    def number(table, name):
        return table.setdefault(name, len(table))

    def send(name, into, src, dst, to):
        pltpu.make_async_remote_copy(
            src_ref=src, dst_ref=dst,
            send_sem=ss.at[number(sends, name)], recv_sem=rs.at[number(receives, into)],
            device_id=to, device_id_type=MESH,
        ).start()

    def wait(name, ref, arrival=True):
        copy = pltpu.make_async_remote_copy(
            src_ref=ref, dst_ref=ref,
            send_sem=ss.at[0 if arrival else number(sends, name)],
            recv_sem=rs.at[number(receives, name) if arrival else 0],
            device_id=across, device_id_type=MESH,
        )
        copy.wait_recv() if arrival else copy.wait_send()

    def left_here(name, ref):
        wait(name, ref, arrival=False)

    def fetch(name, src, dst):
        pltpu.make_async_copy(src, dst, ls.at[number(loads, name)]).start()

    def ready(name, ref):
        pltpu.make_async_copy(ref, ref, ls.at[number(loads, name)]).wait()

    class Gather:
        def __init__(self, name, first, at, half):
            self.name, self.at, self.half = name, at, half
            self.first, self.second = first, "z" if first == "x" else "x"
            self.i, self.j = (x, z) if first == "x" else (z, x)

        def place(self, i, j):
            return self.at(j, i) if self.first == "x" else self.at(i, j)

        def key(self, k):
            return (self.name, k)

        def pass_on(self, axis, by, count, into, ref):
            send(self.key(count), self.key(into), ref, ref, near[axis, by])

        def s0(self):
            ref = self.place(self.i, self.j)
            for by in (1, -1):
                self.pass_on(self.first, by, "f", "a", ref)
            for by in (1, -1):
                self.pass_on(self.second, by, "s", "c0", ref)

        def s1(self):
            wait(self.key("a"), self.place(pl.ds(0, 2), self.j))
            for by, part in ((1, 0), (-1, 1)):
                ref = self.half(self.place(turn(self.i, -by), self.j), part)
                self.pass_on(self.first, by, "f", "b", ref)
            for off in (1, -1):
                ref = self.place(turn(self.i, off), self.j)
                for by in (1, -1):
                    self.pass_on(self.second, by, "s", "c1", ref)

        def s2(self):
            wait(self.key("b"), self.place(self.i, self.j))
            ref = self.place(turn(self.i, 2), self.j)
            for by in (1, -1):
                self.pass_on(self.second, by, "s", "c2", ref)

        def forward(self, i):
            for by, part in ((1, 0), (-1, 1)):
                ref = self.half(self.place(i, turn(self.j, -by)), part)
                self.pass_on(self.second, by, "s", "d", ref)

        def s3(self):
            wait(self.key("c0"), self.place(pl.ds(0, 2), self.j))
            self.forward(self.i)

        def s4(self):
            wait(self.key("c1"), self.place(pl.ds(0, 4), self.j))
            self.forward(turn(self.i, 1))
            self.forward(turn(self.i, -1))

        def s5(self):
            wait(self.key("c2"), self.place(pl.ds(0, 2), self.j))
            self.forward(turn(self.i, 2))

        def end(self):
            wait(self.key("d"), self.place(pl.ds(0, 4), self.j))

        def first_send(self):
            for by, parts in ((1, (0, 1)), (-1, (1, 0))):
                for k, part in enumerate(parts):
                    ref = self.half(self.place(self.i, self.j), part)
                    self.pass_on(self.first, by, "f", "b" if k else "a", ref)

        def first_pass(self):
            wait(self.key("a"), self.place(self.i, self.j))
            for by, part in ((1, 0), (-1, 1)):
                ref = self.half(self.place(turn(self.i, -by), self.j), part)
                self.pass_on(self.first, by, "f", "b", ref)

        def first_end(self):
            wait(self.key("b"), self.place(pl.ds(0, 2), self.j))

        def second_send(self):
            for by, parts in ((1, (0, 1)), (-1, (1, 0))):
                for k, part in enumerate(parts):
                    ref = self.place(pl.ds(2 * part, 2), self.j)
                    self.pass_on(self.second, by, "s", "c1" if k else "c0", ref)

        def second_pass(self):
            wait(self.key("c0"), self.place(pl.ds(0, 4), self.j))
            for by, part in ((1, 0), (-1, 1)):
                ref = self.place(pl.ds(2 * part, 2), turn(self.j, -by))
                self.pass_on(self.second, by, "s", "d", ref)

        def second_end(self):
            wait(self.key("c1"), self.place(pl.ds(0, 4), self.j))
            wait(self.key("d"), self.place(pl.ds(0, 4), self.j))

        def finish(self):
            left_here(self.key("f"), self.place(pl.ds(0, 3), self.j))
            left_here(self.key("s"), self.place(pl.ds(0, 4), pl.ds(0, 3)))

    rows = lambda ref, part: ref.at[..., pl.ds(RI // 2 * part, RI // 2), :]
    slots = lambda ref, part: ref.at[..., pl.ds(part, 1), :, :]
    axes = ("x", "z")

    def pair(make):
        return [make(h) for h in range(2)]

    def q_job(p):
        return pair(lambda h: Gather(("q", p, h), axes[h], lambda zz, xx: qg.at[p, h, zz, xx], rows))

    def p_job(p, k):
        yy = (yhi, other)[k]
        return pair(lambda h: Gather(("p", p, k, h), axes[h], lambda zz, xx: pre.at[p, h, zz, yy, xx], rows))

    qo_job = pair(lambda h: Gather(("qo", h), axes[h], lambda zz, xx: qog.at[h, zz, xx], slots))
    po_job = pair(lambda h: Gather(("po", h), axes[h], lambda zz, xx: preo.at[h, zz, yhi, xx], slots))
    q0_job, q1_job = q_job(0), q_job(1)
    p0_job, p1_job, p0_far, p1_far = p_job(0, 0), p_job(1, 0), p_job(0, 1), p_job(1, 1)

    def do(step, job):
        for gather in job:
            getattr(gather, step)()

    def columns(ref, p, zz, yy, width):
        return ref.at[p, :, pl.ds(pl.multiple_of((zz * 2 + yy) * width, width), width)]

    fetch("qo", qo_hbm, qo_all)
    fetch("q", q_hbm, q_all)
    barrier = pltpu.get_barrier_semaphore()
    peers = list(near.values()) + [across] + mates
    for peer in peers:
        pl.semaphore_signal(barrier, inc=1, device_id=peer, device_id_type=MESH)
    h_own = [hb.at[p, :, pl.ds(0, RI)] for p in range(SLOTS)]
    h_other = [hb.at[p, :, pl.ds(RI, RI)] for p in range(SLOTS)]
    ho_own, ho_other = hob.at[:, :, pl.ds(0, RO)], hob.at[:, :, pl.ds(RO, RO)]
    for p in range(SLOTS):
        for zz in range(4):
            fetch("ho", columns(ho_hbm, p, zz, yhi, 4 * RO), ho_own.at[p, zz])
    for p in range(SLOTS):
        for zz in range(4):
            fetch(("h", p), columns(h_hbm, p, zz, yhi, 4 * RI), h_own[p].at[zz])

    def share_h(p, *some):
        for zz in some or range(4):
            send(("h", p), ("h", p), columns(h_hbm, p, zz, other, 4 * RI), h_other[p].at[zz], across)

    def share_h_out():
        for p in range(SLOTS):
            for zz in range(4):
                send("ho", "ho", columns(ho_hbm, p, zz, other, 4 * RO), ho_other.at[p, zz], across)

    def share_part(p):
        ready(("h", p), h_own[p])
        wait(("h", p), h_other[p])
        for h in range(2):
            def add(zz, acc):
                return acc + dot(hb[p, zz], qg[p, h, zz].reshape(4 * RI, HALF))
            acc = lax.fori_loop(0, 4, add, jnp.zeros((2 * RI, HALF), F32))
            own[p, h] = acc[:RI]
            part_s[p, h] = acc[RI:].astype(BF16)
            send(("part", p), ("part", p, h), part_s.at[p, h], part_r.at[p, h], across)

    def share_pre(p):
        for h in range(2):
            wait(("part", p, h), part_r.at[p, h])
            pre[p, h, z, yhi, x] = (own[p, h] + part_r[p, h].astype(F32)).astype(BF16)
            ref = pre.at[p, h, z, yhi, x]
            send(("y", p), ("y", p), ref, ref, across)

    def got_pre(p):
        wait(("y", p), pre.at[p, :, z, other, x])

    def share_part_out():
        ready("ho", ho_own)
        wait("ho", ho_other)
        for h in range(2):
            for p in range(SLOTS):
                acc = jnp.zeros((2 * RO, HALF), F32)
                for zz in range(4):
                    acc = acc + dot(hob[p, zz], qog[h, zz, :, p].reshape(4 * RO, HALF))
                owno[h, p] = acc[:RO]
                parto_s[h, p] = acc[RO:].astype(BF16)
        send("parto", "parto", parto_s, parto_r, across)

    def make_pre_out():
        wait("parto", parto_r)
        for h in range(2):
            preo[h, z, yhi, x] = (owno[h] + parto_r[h].astype(F32)).astype(BF16)

    def share_pre_out():
        for h in range(2):
            ref = preo.at[h, :, yhi]
            send("yo", "yo", ref, ref, across)

    def make_left(p, yy, fresh):
        k = pl.ds(pl.multiple_of(yy * 4 * RI, 4 * RI), 4 * RI)
        for h in range(2):
            def part(zz):
                return dot(acts[p, zz, :, k], pre[p, h, zz, yy].reshape(4 * RI, HALF))

            def add(zz, carry):
                left[p, h] += part(zz)
                return carry

            if fresh:
                left[p, h] = part(0)
            lax.fori_loop(1 if fresh else 0, 4, add, 0)

    def got_acts(p):
        ready(("a", p), acts.at[p])

    def make_right():
        ready("g", grads)
        wait("yo", preo.at[:, :, other])
        for p in range(SLOTS):
            for h in range(2):
                right[p, h] = dot(grads[p], preo[h, :, :, :, p].reshape(DOUT, HALF))

    def place_q(p):
        m = order[group * SLOTS + p]
        for h in range(2):
            qg[p, h, z, x] = q_all[m, :, pl.ds(h * HALF, HALF)]

    def place_q_out():
        for p in range(SLOTS):
            m = order[group * SLOTS + p]
            for h in range(2):
                qog[h, z, x, p] = qo_all[m, :, pl.ds(h * HALF, HALF)]

    def load_rest():
        for p in range(SLOTS):
            for zz in range(4):
                fetch(("a", p), a_hbm.at[p, :, pl.ds(zz * 8 * RI, 8 * RI)], acts.at[p, zz])
        fetch("g", g_hbm, grads)

    schedule = [
        (pl.semaphore_wait, barrier, len(peers)),
        (share_h_out,),
        (share_h, 0),
        (share_h, 1, 0),
        (ready, "qo", qo_all),
        (place_q_out,),
        (do, "s0", qo_job),
        (ready, "q", q_all),
        (place_q, 0),
        (do, "first_send", q0_job),
        (place_q, 1),
        (do, "s3", qo_job),
        (do, "s1", qo_job),
        (do, "first_pass", q0_job),
        (do, "first_send", q1_job),
        (load_rest,),
        (do, "s2", qo_job),
        (do, "s4", qo_job),
        (do, "first_end", q0_job),
        (do, "second_send", q0_job),
        (do, "first_pass", q1_job),
        (do, "s5", qo_job),
        (do, "second_pass", q0_job),
        (do, "first_end", q1_job),
        (do, "second_send", q1_job),
        (do, "end", qo_job),
        (share_part_out,),
        (do, "second_end", q0_job),
        (share_part, 0),
        (make_pre_out,),
        (do, "s0", po_job),
        (do, "second_pass", q1_job),
        (share_pre, 0),
        (share_h, 1, 1),
        (share_h, 1, 2),
        (share_h, 1, 3),
        (do, "first_send", p0_job),
        (do, "s1", po_job),
        (do, "s3", po_job),
        (do, "second_end", q1_job),
        (do, "first_pass", p0_job),
        (got_pre, 0),
        (do, "s0", p0_far),
        (do, "s2", po_job),
        (do, "s4", po_job),
        (do, "first_end", p0_job),
        (do, "second_send", p0_job),
        (do, "s1", p0_far),
        (do, "s5", po_job),
        (do, "s3", p0_far),
        (do, "second_pass", p0_job),
        (share_part, 1),
        (share_pre, 1),
        (do, "s0", p1_job),
        (do, "end", po_job),
        (do, "s2", p0_far),
        (do, "s4", p0_far),
        (share_pre_out,),
        (do, "second_end", p0_job),
        (got_acts, 0),
        (got_acts, 1),
        (make_left, 0, yhi, True),
        (got_pre, 1),
        (do, "first_send", p1_far),
        (do, "s1", p1_job),
        (do, "s3", p1_job),
        (do, "s5", p0_far),
        (do, "first_pass", p1_far),
        (do, "s2", p1_job),
        (do, "s4", p1_job),
        (do, "end", p0_far),
        (make_left, 0, other, False),
        (do, "first_end", p1_far),
        (do, "second_send", p1_far),
        (do, "s5", p1_job),
        (make_right,),
        (do, "second_pass", p1_far),
        (do, "end", p1_job),
        (make_left, 1, yhi, True),
        (do, "second_end", p1_far),
        (make_left, 1, other, False),
    ]
    for step, *given in schedule:
        step(*given)

    r = lax.broadcasted_iota(jnp.int32, (16, HALF), 0)
    c = lax.broadcasted_iota(jnp.int32, (16, HALF), 1)
    first = c // 32 * 2 - c // 128 * 8
    pick = (r // 8 == c // 128) & ((r - r // 8 * 8) * 2 == first)
    pick = jnp.where(pick, 1.0, 0.0).astype(F32)
    for h in range(2):
        product = left[0, h] * right[0, h] + left[1, h] * right[1, h]
        sums = lax.dot_general(
            pick, product, (((1,), (1,)), ((), ())),
            precision=lax.Precision.HIGHEST, preferred_element_type=F32,
        )
        score[pl.ds(2 * h, 2)] = sums.reshape(2, 8, TOK)
    for k, mate in enumerate(mates):
        send("score", "score", score.at[mate[0]], score_r.at[k], mate)
    wait("score", score_r)
    out[...] = (score[group] + score_r[0]) + (score_r[1] + score_r[2])

    for job in [qo_job, po_job, q0_job, q1_job, p0_job, p1_job, p0_far, p1_far]:
        do("finish", job)
    for p in range(SLOTS):
        left_here(("h", p), h_other[p])
        left_here(("part", p), part_s.at[p])
        left_here(("y", p), pre.at[p, :, z, yhi, x])
    left_here("ho", ho_other)
    left_here("parto", parto_s)
    left_here("yo", preo.at[:, :, yhi])
    left_here("score", score_r)
    assert (len(sends), len(receives), len(loads)) == (SENDS, RECEIVES, LOADS), len(receives)


def shards(input_acts, output_grads, input_inverse, output_inverse, query_input, query_output, layer_order):
    any_space = pl.BlockSpec(memory_space=pl.ANY)
    result = pl.pallas_call(
        kernel,
        out_shape=jax.ShapeDtypeStruct((8, TOK), F32),
        in_specs=[pl.BlockSpec(memory_space=pltpu.SMEM)] + [any_space] * 6,
        out_specs=pl.BlockSpec(memory_space=pltpu.VMEM),
        scratch_shapes=[
            pltpu.VMEM((8, RI, WIDTH), BF16),
            pltpu.VMEM((8, RO, WIDTH), BF16),
            pltpu.VMEM((SLOTS, 2, 4, 4, RI, HALF), BF16),
            pltpu.VMEM((2, 4, 4, SLOTS, RO, HALF), BF16),
            pltpu.VMEM((SLOTS, 4, 2 * RI, 4 * RI), BF16),
            pltpu.VMEM((SLOTS, 4, 2 * RO, 4 * RO), BF16),
            pltpu.VMEM((SLOTS, 2, RI, HALF), BF16),
            pltpu.VMEM((SLOTS, 2, RI, HALF), BF16),
            pltpu.VMEM((2, SLOTS, RO, HALF), BF16),
            pltpu.VMEM((2, SLOTS, RO, HALF), BF16),
            pltpu.VMEM((SLOTS, 2, RI, HALF), F32),
            pltpu.VMEM((2, SLOTS, RO, HALF), F32),
            pltpu.VMEM((SLOTS, 2, 4, 2, 4, RI, HALF), BF16),
            pltpu.VMEM((2, 4, 2, 4, SLOTS, RO, HALF), BF16),
            pltpu.VMEM((SLOTS, 4, TOK, 8 * RI), BF16),
            pltpu.VMEM((SLOTS, TOK, DOUT), BF16),
            pltpu.VMEM((SLOTS, 2, TOK, HALF), F32),
            pltpu.VMEM((SLOTS, 2, TOK, HALF), F32),
            pltpu.VMEM((4, 8, TOK), F32),
            pltpu.VMEM((3, 8, TOK), F32),
            pltpu.SemaphoreType.DMA((SENDS,)),
            pltpu.SemaphoreType.DMA((RECEIVES,)),
            pltpu.SemaphoreType.DMA((LOADS,)),
        ],
        compiler_params=pltpu.CompilerParams(
            collective_id=0, has_side_effects=True, vmem_limit_bytes=56 * 2**20
        ),
    )(layer_order, query_input, query_output, input_acts, output_grads, input_inverse, output_inverse)
    return result[:4].T


def solution(mesh):
    in_specs = (
        P("layer", "shard", None),
        P("layer", "shard", None),
        P("layer", "shard", None),
        P("layer", "shard", None),
        P(None, "shard", None),
        P(None, "shard", None),
        P(),
    )
    return jax.shard_map(shards, mesh=mesh, in_specs=in_specs, out_specs=P("shard", "layer"), check_vma=False)
```
